32 devices in a mesh: les: 4 (over y, x), ac: 8 (over z, core).
Axes of the slice: x: 2, y: 2, z: 4, core: 2. Of those that a mesh axis runs over, the one named last changes fastest.
Arguments:
- velocity: bfloat16 [3, 32768, 128], P(None, ('les', 'ac')), may hold values from -6 to 6
- vorticity: bfloat16 [3, 32768, 128], P(None, ('les', 'ac')), may hold values from -6 to 6
- cover: int32 [32768, 2], P(('les', 'ac')), may hold values from 0 to 31, all different within a row; in each aligned block of 1024 rows (0 to 1023, 1024 to 2047, ...) at most 128 rows name the same one
- target_line: int32 [32768, 2], P(('les', 'ac')), may hold values from 0 to 511
- phase: int32 [32768, 2], P(('les', 'ac')), may hold values from 0 to 3
- fringe_lines: int32 [32, 2], P(('les', 'ac')), may hold values from 0 to 511
- acoustic: float32 [4, 16384, 256], P(None, ('les', 'ac')), may hold values from -6 to 6
Outputs:
- acoustic_next: float32 [4, 16384, 256], P(None, ('les', 'ac'))
The draws below stay inside these ranges and needn't reach their ends.
Inputs may be any that keep to these rules, and one draw needn't show every extreme that they name: `cover`: within the rows of one device, no acoustic block is named more than 128 times, and some block exactly 128 times; the 2 blocks of one slab differ.
All inputs are finite; a program needn't handle non-finite values.
Results may differ from the reference program's by a relative error of at most 0.003.
Values may be sent and summed in bfloat16 or wider, within the bound.
A program may use at most 64 MiB of HBM per device.

```python
import math
import jax
import jax.numpy as jnp
import numpy as np
from jax import lax

SLAB_CELLS = 128
CELLS = 256
NOFF = 4
TOP = 2
SLAB_DEV = 1024
LINES = 512
SLABS = 32768
NBLK = 32
CAP = 128
ROWS = 16384
N_LES = 4
N_AC = 8


def touch_ends(array, rng, low, top_value):
    place = [jax.random.randint(jax.random.fold_in(rng, axis), (), 0, length) for axis, length in enumerate(array.shape)]
    longest = array.shape.index(max(array.shape))
    next_to = place[:longest] + [(place[longest] + 1) % array.shape[longest]] + place[longest + 1:]
    return array.at[tuple(place)].set(low).at[tuple(next_to)].set(top_value)


def steps_of(rng, dims, shards, smallest, top_value):
    level, own = 1.0, jax.random.fold_in(rng, 6)
    for axis_at, shards_of in shards:
        steps = jnp.exp(jax.random.uniform(jax.random.fold_in(own, axis_at), (shards_of,), jnp.float32, smallest / len(shards), top_value / len(shards)))
        level = level * jnp.repeat(steps, dims[axis_at] // shards_of).reshape([-1 if axis == axis_at else 1 for axis in range(len(dims))])
    return level


def assign_block(stream_key, own, number, rows, count, top, reach, skew):
    ranking = jax.random.permutation(stream_key, count)
    crowded, ordinary = portions_of(count, rows * top, reach, skew, True), portions_of(count, rows * top, reach, skew, False)
    places = jnp.arange(count)

    def named(sizes, turn):
        used = int((sizes > 0).sum())
        fixed = max(1, used // 4)
        moved = fixed + (places - fixed + turn * (used - fixed)) % max(1, count - fixed)
        return jnp.zeros((count,), jnp.int32).at[ranking[jnp.where(places < fixed, places, moved)]].set(jnp.asarray(sizes, jnp.int32))

    sizes = jnp.where(number % 4 == 0, named(crowded, number // 4), named(ordinary, number - number // 4 - 1))
    mixed = jax.random.permutation(jax.random.fold_in(own, 3), count)
    giver, receiver = mixed[0:count // 2 * 2:2], mixed[1:count // 2 * 2:2]
    room = jnp.minimum(sizes[giver] - 1, reach - sizes[receiver]) // 2
    room = jnp.where((giver == ranking[0]) | (receiver == ranking[0]) | (sizes[receiver] == 0), 0, jnp.maximum(room, 0))
    moved = jax.random.randint(jax.random.fold_in(own, 4), (count // 2,), 0, 1 << 20) % (room + 1)
    sizes = sizes.at[giver].add(-moved).at[receiver].add(moved)
    labels = jnp.searchsorted(jnp.cumsum(sizes), jnp.arange(rows * top), side="right").astype(jnp.int32)
    table = labels.reshape(top, rows).T
    table = table[jax.random.permutation(jax.random.fold_in(own, 1), rows)]
    turn = jax.random.randint(jax.random.fold_in(own, 2), (rows, 1), 0, top)
    return jnp.take_along_axis(table, (jnp.arange(top)[None, :] + turn) % top, axis=1)


def portions_of(amount, total, limit, skew, full):
    portions = [(1 << 20) // math.isqrt(grade ** skew) + 1 for grade in range(1, amount + 1)]
    largest = limit if full else min(limit, max(-(-total // amount), total * portions[0] // sum(portions)))
    least = 1 if total - largest >= amount - 1 else 0
    counts, rest = [largest] + [least] * (amount - 1), total - largest - least * (amount - 1)
    while rest > 0:
        movable = [i for i in range(1, amount) if counts[i] < largest] or [i for i in range(1, amount) if counts[i] < limit]
        pool, left = sum([portions[i] for i in movable]), rest
        for i in movable:
            addition = min(limit - counts[i], max(1, left * portions[i] // pool), rest)
            counts[i] = counts[i] + addition
            rest = rest - addition
    return np.array(counts)


def noise(key, shape, deviation, reach, shards=(), held_as=jnp.bfloat16):
    array = jax.random.normal(key, shape, jnp.float32) * deviation
    if len(shards) > 0:
        array = steps_of(key, shape, shards, -0.22, 0.18) * array
    return jnp.clip(array, min=-reach, max=reach).astype(held_as)


def setup_inputs(seed: int = 0) -> dict:
    key_of = jax.random.split(jax.random.key(seed), 8)
    velocity = noise(key_of[0], (3, SLABS, SLAB_CELLS), 1.0, 6.0, ((1, 32),))
    vorticity = noise(key_of[1], (3, SLABS, SLAB_CELLS), 1.0, 6.0, ((1, 32),))
    cover_keys = jax.random.split(jax.random.fold_in(key_of[2], 1), SLABS // SLAB_DEV)
    cover_turns = jax.random.permutation(jax.random.fold_in(key_of[2], 3), SLABS // SLAB_DEV)
    cover = jax.vmap(lambda own, number: assign_block(jax.random.fold_in(key_of[2], 2), own, number, SLAB_DEV, NBLK, TOP, CAP, 2))(cover_keys, cover_turns).reshape((SLABS, TOP))
    target_line = touch_ends(jax.random.randint(key_of[3], (SLABS, TOP), 0, LINES), jax.random.fold_in(key_of[3], 1), 0, LINES - 1).astype(jnp.int32)
    phase = touch_ends(jax.random.randint(key_of[4], (SLABS, TOP), 0, NOFF), jax.random.fold_in(key_of[4], 1), 0, NOFF - 1).astype(jnp.int32)
    fringe_lines = touch_ends(jax.random.randint(key_of[5], (NBLK, 2), 0, LINES), jax.random.fold_in(key_of[5], 1), 0, LINES - 1).astype(jnp.int32)
    acoustic = noise(key_of[6], (4, ROWS, CELLS), 1.0, 6.0, ((1, 32),), jnp.float32)
    return {"velocity": velocity, "vorticity": vorticity, "cover": cover, "target_line": target_line, "phase": phase, "fringe_lines": fringe_lines, "acoustic": acoustic}


ADVECT = 0.5
STEP = 0.4

def lagrange_table(coarse, fine, phases):
    fine_ids = jnp.arange(fine, dtype=jnp.int32)
    phase_ids = jnp.arange(phases, dtype=jnp.int32)
    numerator = phases * fine_ids[None, :] + phase_ids[:, None]
    first_tap = jnp.clip(numerator // (2 * phases) - 1, 0, coarse - 4)
    where_x = numerator.astype(jnp.float32) / (2.0 * phases)
    coarse_ids = jnp.arange(coarse, dtype=jnp.int32)
    lagrange = jnp.zeros((phases, coarse, fine), jnp.float32)
    for tap_index in range(4):
        weight = jnp.ones_like(where_x)
        for other_tap in range(4):
            if other_tap != tap_index:
                weight = weight * (where_x - (first_tap + other_tap).astype(jnp.float32)) / float(tap_index - other_tap)
        hit_mask = coarse_ids[None, :, None] == (first_tap + tap_index)[:, None, :]
        lagrange = lagrange + jnp.where(hit_mask, weight[:, None, :], jnp.float32(0.0))
    return lagrange

def derivative_matrix(cells):
    cell_ids = np.arange(cells)
    distance = cell_ids[:, None] - cell_ids[None, :]
    rhs_matrix = jnp.asarray(np.where(distance == -1, 0.75, np.where(distance == 1, -0.75, 0.0)), dtype=jnp.float32)
    main_band = jnp.ones((cells,), jnp.float32)
    lower_band = jnp.asarray(np.where(cell_ids == 0, 0.0, 0.25), dtype=jnp.float32)
    upper_band = jnp.asarray(np.where(cell_ids == cells - 1, 0.0, 0.25), dtype=jnp.float32)
    solved = lax.linalg.tridiagonal_solve(lower_band, main_band, upper_band, rhs_matrix)
    return solved.T

def ape_rates(dx_all, dy_pressure, dy_across, source):
    pressure = -ADVECT * dx_all[0] - dx_all[1] - dy_across
    along = -ADVECT * dx_all[1] - dx_all[0] - source[0]
    across = -ADVECT * dx_all[2] - dy_pressure - source[1]
    spanwise = -ADVECT * dx_all[3] - source[2]
    return jnp.stack([pressure, along, across, spanwise])

def reference(velocity, vorticity, cover, target_line, phase, fringe_lines, acoustic):
    lamb = jnp.cross(vorticity.astype(jnp.float32), velocity.astype(jnp.float32), axis=0).astype(jnp.bfloat16)
    slab_rows = jnp.transpose(lamb, (1, 0, 2)).reshape(SLABS, 3 * SLAB_CELLS)
    weights = lagrange_table(SLAB_CELLS, CELLS, NOFF).astype(jnp.bfloat16)

    def add_block(total, block_index):
        start = (block_index * SLAB_DEV).astype(jnp.int32)
        rows_here = lax.dynamic_slice_in_dim(slab_rows, start, SLAB_DEV, 0).astype(jnp.float32)
        blocks_here = lax.dynamic_slice_in_dim(cover, start, SLAB_DEV, 0)
        lines_here = lax.dynamic_slice_in_dim(target_line, start, SLAB_DEV, 0)
        phases_here = lax.dynamic_slice_in_dim(phase, start, SLAB_DEV, 0)
        for column in range(TOP):
            segment = (blocks_here[:, column] * LINES + lines_here[:, column]) * NOFF + phases_here[:, column]
            total = total.at[segment].add(rows_here)
        return (total, None)
    initial = jnp.zeros((NBLK * LINES * NOFF, 3 * SLAB_CELLS), jnp.float32)
    total, _ = lax.scan(add_block, initial, jnp.arange(SLABS // SLAB_DEV, dtype=jnp.int32))
    gathered = total.astype(jnp.bfloat16).reshape(NBLK * LINES, NOFF, 3, SLAB_CELLS)
    source_flat = jnp.einsum('rock,okj->crj', gathered.astype(jnp.float32), weights.astype(jnp.float32))
    source = source_flat.reshape(3, N_LES, N_AC, LINES, CELLS)
    dmat = derivative_matrix(CELLS)
    fringe = fringe_lines.reshape(N_LES, N_AC, 2)

    def face_of(field, column):
        index_grid = jnp.broadcast_to(fringe[:, :, column][:, :, None, None], (N_LES, N_AC, 1, CELLS))
        return jnp.take_along_axis(field, index_grid, axis=2)[:, :, 0, :]

    def y_rate(field, column_up, column_down):
        up_face = face_of(field, column_up)
        down_face = face_of(field, column_down)
        zero_face = jnp.zeros_like(up_face[:, :1])
        low_ghost = jnp.concatenate([zero_face, up_face[:, :-1]], axis=1)
        high_ghost = jnp.concatenate([down_face[:, 1:], zero_face], axis=1)
        extended = jnp.concatenate([low_ghost[:, :, None], field, high_ghost[:, :, None]], axis=2)
        return (extended[:, :, 2:] - extended[:, :, :-2]) * 0.5

    def tendency(state):
        dx_all = jnp.dot(state.reshape(-1, CELLS), dmat, precision=lax.Precision.HIGHEST).reshape(state.shape)
        dy_pressure = y_rate(state[0], 0, 1)
        dy_across = y_rate(state[2], 0, 1)
        return ape_rates(dx_all, dy_pressure, dy_across, source)
    state = acoustic.reshape(4, N_LES, N_AC, LINES, CELLS)
    first = tendency(state)
    second = tendency(state + 0.5 * STEP * first)
    third = tendency(state + 0.5 * STEP * second)
    fourth = tendency(state + STEP * third)
    result = state + STEP / 6.0 * (first + 2.0 * second + 2.0 * third + fourth)
    return result.reshape(4, ROWS, CELLS)
```

```python
import functools

import jax
import jax.numpy as jnp
import ml_dtypes
import numpy as np
from jax import lax
from jax.experimental import pallas as pl
from jax.experimental.pallas import tpu as pltpu
from jax.sharding import PartitionSpec as P

NOFF = 4
ADVECT = 0.5
STEP = 0.4
MESH = pl.DeviceIdType.MESH
VMEM_LIMIT = 60 * 1024 * 1024


def lagrange_table(coarse, fine, phases):
    fine_ids = np.arange(fine)
    phase_ids = np.arange(phases)
    numerator = phases * fine_ids[None, :] + phase_ids[:, None]
    first_tap = np.clip(numerator // (2 * phases) - 1, 0, coarse - 4)
    where_x = numerator / (2.0 * phases)
    lagrange = np.zeros((phases, coarse, fine))
    for tap in range(4):
        weight = np.ones_like(where_x)
        for other in range(4):
            if other != tap:
                weight = weight * (where_x - (first_tap + other)) / float(tap - other)
        hit = np.arange(coarse)[None, :, None] == (first_tap + tap)[:, None, :]
        lagrange = lagrange + np.where(hit, weight[:, None, :], 0.0)
    return lagrange.astype(np.float32).astype(ml_dtypes.bfloat16)


def derivative_matrix(cells):
    ids = np.arange(cells)
    distance = ids[:, None] - ids[None, :]
    rhs = np.where(distance == -1, 0.75, np.where(distance == 1, -0.75, 0.0))
    lhs = np.where(distance == 0, 1.0, np.where(np.abs(distance) == 1, 0.25, 0.0))
    return np.linalg.solve(lhs, rhs).T.astype(np.float32).astype(ml_dtypes.bfloat16)


def dot(a, b):
    return jnp.dot(a, b, preferred_element_type=jnp.float32)


def prep_kernel(devices, capacity, vel_ref, vort_ref, index_ref, rows_ref, codes_ref,
                lamb_ref, rank_ref, tag_ref):
    slabs = vel_ref.shape[1]
    coarse = vel_ref.shape[2]
    vel = [vel_ref[c].astype(jnp.float32) for c in range(3)]
    vor = [vort_ref[c].astype(jnp.float32) for c in range(3)]
    for c in range(3):
        a, b = (c + 1) % 3, (c + 2) % 3
        lamb_ref[:, c * coarse:(c + 1) * coarse] = (
            vor[a] * vel[b] - vor[b] * vel[a]).astype(jnp.bfloat16)
    block = lax.broadcasted_iota(jnp.int32, (devices, slabs), 0)
    first = block == index_ref[0:1, :]
    second = block == index_ref[1:2, :]
    hit = first | second
    hit_f = jnp.where(hit, 1.0, 0.0)
    tag_ref[...] = jnp.where(first, index_ref[2:3, :], jnp.where(second, index_ref[3:4, :], 0))
    width = 128
    above = (lax.broadcasted_iota(jnp.int32, (width, width), 0)
             < lax.broadcasted_iota(jnp.int32, (width, width), 1))
    above = jnp.where(above, 1.0, 0.0).astype(jnp.bfloat16)
    offset = jnp.zeros((devices, 1), jnp.float32)
    for k in range(slabs // width):
        part = hit_f[:, k * width:(k + 1) * width]
        rank = dot(part.astype(jnp.bfloat16), above) + offset
        rank_ref[:, k * width:(k + 1) * width] = jnp.where(part > 0.5, rank, -1.0).astype(jnp.int32)
        offset = offset + jnp.sum(part, axis=1, keepdims=True)
    group = 512
    per = group // capacity
    slot = lax.broadcasted_iota(jnp.int32, (capacity, slabs), 0)

    def step(k, carry):
        code_rows = []
        pieces = []
        for q in range(per):
            d = k * per + q
            match = slot == rank_ref[pl.ds(d, 1), :]
            one = jnp.where(match, 1.0, 0.0).astype(jnp.bfloat16)
            pieces.append(one)
            tag = tag_ref[pl.ds(d, 1), :]
            tag = jnp.concatenate([(tag // 32 + 1), tag % 32] + [jnp.zeros_like(tag)] * 6, axis=0)
            found = lax.dot_general(
                tag.astype(jnp.float32).astype(jnp.bfloat16), one, (((1,), (1,)), ((), ())),
                preferred_element_type=jnp.float32)
            code_rows.append(found[0:1] * 32.0 + found[1:2] - 32.0)
        one = jnp.concatenate(pieces, axis=0)
        rows_ref[pl.ds(k * group, group), :] = dot(one, lamb_ref[...]).astype(jnp.bfloat16)
        codes_ref[pl.ds(k, 1), :] = jnp.concatenate(code_rows, axis=1).astype(jnp.int32)
        return carry

    lax.fori_loop(0, devices * capacity // group, step, 0)


def step_kernel(lines_ref, rows_ref, codes_ref, weights_ref, dmat_ref, state_ref, out_ref,
                source_ref, stage_ref, dx_ref, sum_ref, send_ref, ghost_ref,
                send_sem, recv_sem):
    n_ac = lax.axis_size("ac")
    me = lax.axis_index("ac")
    lines = state_ref.shape[1]
    cells = state_ref.shape[2]
    coarse = weights_ref.shape[1]
    pad = 8
    ghost_ref[...] = jnp.zeros_like(ghost_ref)
    send_ref[...] = jnp.zeros_like(send_ref)
    barrier = pltpu.get_barrier_semaphore()

    for near in (lax.rem(me + 1, n_ac), lax.rem(me + n_ac - 1, n_ac)):
        pl.semaphore_signal(barrier, inc=1, device_id={"ac": near}, device_id_type=MESH)

    chunk = 256
    slots = rows_ref.shape[0]

    def combine(k, carry):
        for o in range(NOFF):
            target = lax.broadcasted_iota(jnp.int32, (chunk, slots), 0) + (o * lines + k * chunk)
            one = jnp.where(target == codes_ref[...], 1.0, 0.0).astype(jnp.bfloat16)
            got = dot(one, rows_ref[...]).astype(jnp.bfloat16)
            for c in range(3):
                value = dot(got[:, c * coarse:(c + 1) * coarse], weights_ref[o])
                at = (c, pl.ds(k * chunk, chunk))
                if o == 0:
                    source_ref[at] = value
                else:
                    source_ref[at] += value
        return carry

    lax.fori_loop(0, lines // chunk, combine, 0)

    pl.semaphore_wait(barrier, 2)
    up_line = lines_ref[0, 0]
    down_line = lines_ref[0, 1]
    scale_in = (None, 0.5 * STEP, 0.5 * STEP, STEP)
    scale_out = (STEP / 6.0, STEP / 3.0, STEP / 3.0, STEP / 6.0)
    for f in range(4):
        stage_ref[f, pad:pad + lines, :] = state_ref[f]
    for s in range(4):
        for q, f in enumerate((0, 2)):
            send_ref[s, 0, q:q + 1, :] = stage_ref[f, pl.ds(pad + up_line, 1), :]
            send_ref[s, 1, q:q + 1, :] = stage_ref[f, pl.ds(pad + down_line, 1), :]

        def copy(side, to):
            return pltpu.make_async_remote_copy(
                src_ref=send_ref.at[s, side], dst_ref=ghost_ref.at[s, side],
                send_sem=send_sem.at[s, side], recv_sem=recv_sem.at[s, side],
                device_id={"ac": to}, device_id_type=MESH)

        def dx_of(f):
            dx_ref[f] = dot(stage_ref[f, pad:pad + lines, :].astype(jnp.bfloat16), dmat_ref[...])

        dx_of(0)

        @pl.when(me < n_ac - 1)
        def _():
            copy(0, me + 1).start()

        @pl.when(me > 0)
        def _():
            copy(1, me - 1).start()

        for f in range(1, 4):
            dx_of(f)

        @pl.when(me < n_ac - 1)
        def _():
            copy(0, me + 1).wait_send()
            copy(1, me + 1).wait_recv()

        @pl.when(me > 0)
        def _():
            copy(1, me - 1).wait_send()
            copy(0, me - 1).wait_recv()

        for q, f in enumerate((0, 2)):
            stage_ref[f, pad - 1:pad, :] = ghost_ref[s, 0, q:q + 1, :]
            stage_ref[f, pad + lines:pad + lines + 1, :] = ghost_ref[s, 1, q:q + 1, :]

        def dy(f):
            return (stage_ref[f, pad + 1:pad + 1 + lines, :]
                    - stage_ref[f, pad - 1:pad - 1 + lines, :]) * 0.5

        dy_p = dy(0)
        dy_v = dy(2)

        def finish(f, rate):
            if s == 0:
                total = state_ref[f] + scale_out[s] * rate
            else:
                total = sum_ref[f] + scale_out[s] * rate
            if s == 3:
                out_ref[f] = total
            else:
                sum_ref[f] = total
                stage_ref[f, pad:pad + lines, :] = state_ref[f] + scale_in[s + 1] * rate

        finish(0, -ADVECT * dx_ref[0] - dx_ref[1] - dy_v)
        finish(2, -ADVECT * dx_ref[2] - dy_p - source_ref[1])
        finish(1, -ADVECT * dx_ref[1] - dx_ref[0] - source_ref[0])
        finish(3, -ADVECT * dx_ref[3] - source_ref[2])


def local(velocity, vorticity, cover, target_line, phase, fringe_lines, acoustic):
    devices = lax.axis_size("les") * lax.axis_size("ac")
    slabs, coarse = velocity.shape[1:]
    tops = cover.shape[1]
    lines, cells = acoustic.shape[1:]
    capacity = 2 * slabs * tops // devices
    slots = devices * capacity
    index = jnp.concatenate([cover, phase * lines + target_line], axis=1).T
    vmem = pl.BlockSpec(memory_space=pltpu.VMEM)
    rows, codes = pl.pallas_call(
        functools.partial(prep_kernel, devices, capacity),
        out_shape=(jax.ShapeDtypeStruct((slots, 3 * coarse), jnp.bfloat16),
                   jax.ShapeDtypeStruct((slots // 512, 512), jnp.int32)),
        in_specs=[vmem] * 3,
        out_specs=(vmem, vmem),
        scratch_shapes=[pltpu.VMEM((slabs, 3 * coarse), jnp.bfloat16),
                        pltpu.VMEM((devices, slabs), jnp.int32),
                        pltpu.VMEM((devices, slabs), jnp.int32)],
        compiler_params=pltpu.CompilerParams(vmem_limit_bytes=VMEM_LIMIT),
        name="prep",
    )(velocity, vorticity, index)
    codes = lax.all_to_all(codes.reshape(devices, capacity), ("les", "ac"), 0, 0, tiled=True)
    rows = lax.all_to_all(rows, ("les", "ac"), 0, 0, tiled=True)
    return pl.pallas_call(
        step_kernel,
        out_shape=jax.ShapeDtypeStruct(acoustic.shape, jnp.float32),
        in_specs=[pl.BlockSpec(memory_space=pltpu.SMEM)] + [vmem] * 5,
        out_specs=vmem,
        scratch_shapes=[pltpu.VMEM((3, lines, cells), jnp.float32),
                        pltpu.VMEM((4, lines + 16, cells), jnp.float32),
                        pltpu.VMEM((4, lines, cells), jnp.float32),
                        pltpu.VMEM((4, lines, cells), jnp.float32),
                        pltpu.VMEM((4, 2, 8, cells), jnp.float32),
                        pltpu.VMEM((4, 2, 8, cells), jnp.float32),
                        pltpu.SemaphoreType.DMA((4, 2)),
                        pltpu.SemaphoreType.DMA((4, 2))],
        compiler_params=pltpu.CompilerParams(
            vmem_limit_bytes=VMEM_LIMIT, collective_id=0, has_side_effects=True),
        name="step",
    )(fringe_lines, rows, codes.reshape(1, slots), jnp.asarray(lagrange_table(coarse, cells, NOFF)),
      jnp.asarray(derivative_matrix(cells)), acoustic)


def solution(mesh):
    return jax.shard_map(
        local,
        mesh=mesh,
        in_specs=(
            P(None, ("les", "ac"), None),
            P(None, ("les", "ac"), None),
            P(("les", "ac"), None),
            P(("les", "ac"), None),
            P(("les", "ac"), None),
            P(("les", "ac"), None),
            P(None, ("les", "ac"), None),
        ),
        out_specs=P(None, ("les", "ac"), None),
        check_vma=False,
    )
```

```python
import functools

import jax
import jax.numpy as jnp
import ml_dtypes
import numpy as np
from jax import lax
from jax.experimental import pallas as pl
from jax.experimental.pallas import tpu as pltpu
from jax.sharding import PartitionSpec as P

NOFF = 4
ADVECT = 0.5
STEP = 0.4
MESH = pl.DeviceIdType.MESH
VMEM_LIMIT = 60 * 1024 * 1024


def lagrange_table(coarse, fine, phases):
    fine_ids = np.arange(fine)
    phase_ids = np.arange(phases)
    numerator = phases * fine_ids[None, :] + phase_ids[:, None]
    first_tap = np.clip(numerator // (2 * phases) - 1, 0, coarse - 4)
    where_x = numerator / (2.0 * phases)
    lagrange = np.zeros((phases, coarse, fine))
    for tap in range(4):
        weight = np.ones_like(where_x)
        for other in range(4):
            if other != tap:
                weight = weight * (where_x - (first_tap + other)) / float(tap - other)
        hit = np.arange(coarse)[None, :, None] == (first_tap + tap)[:, None, :]
        lagrange = lagrange + np.where(hit, weight[:, None, :], 0.0)
    return lagrange.astype(np.float32).astype(ml_dtypes.bfloat16)


def derivative_matrix(cells):
    ids = np.arange(cells)
    distance = ids[:, None] - ids[None, :]
    rhs = np.where(distance == -1, 0.75, np.where(distance == 1, -0.75, 0.0))
    lhs = np.where(distance == 0, 1.0, np.where(np.abs(distance) == 1, 0.25, 0.0))
    return np.linalg.solve(lhs, rhs).T.astype(np.float32).astype(ml_dtypes.bfloat16)


def dot(a, b):
    return jnp.dot(a, b, preferred_element_type=jnp.float32)


def step_kernel(capacity, lines_ref, vel_ref, vort_ref, index_ref, weights_ref, dmat_ref, state_ref,
                out_ref, source_ref, stage_ref, dx_ref, sum_ref, send_ref, ghost_ref,
                block_ref, table_ref, pack_ref, tags_ref, rows_ref, got_ref, codes_ref,
                rank_ref, tag_ref, send_sem, recv_sem,
                block_send, block_recv, table_send, table_recv,
                rows_send, rows_recv, tags_send, tags_recv):
    n_les = lax.axis_size("les")
    n_ac = lax.axis_size("ac")
    n_chip = n_ac // 2
    here = lax.axis_index("les")
    me = lax.axis_index("ac")
    chip = me // 2
    core = lax.rem(me, 2)
    lines = state_ref.shape[1]
    cells = state_ref.shape[2]
    slabs = vel_ref.shape[1]
    coarse = weights_ref.shape[1]
    plane = 2 * n_les
    pad = 8
    ghost_ref[...] = jnp.zeros_like(ghost_ref)
    send_ref[...] = jnp.zeros_like(send_ref)
    vel = [vel_ref[c].astype(jnp.float32) for c in range(3)]
    vor = [vort_ref[c].astype(jnp.float32) for c in range(3)]
    for c in range(3):
        a, b = (c + 1) % 3, (c + 2) % 3
        block_ref[chip, :, c * coarse:(c + 1) * coarse] = (
            vor[a] * vel[b] - vor[b] * vel[a]).astype(jnp.bfloat16)
    table_ref[chip] = index_ref[...]

    def peer(r):
        return lax.rem(here + r // 2, n_les), lax.rem(core + r % 2, 2)

    barrier = pltpu.get_barrier_semaphore()
    partners = []
    for r in range(1, plane):
        i, c = peer(r)
        partners.append((i, 2 * chip + c))
    for step in (1, n_chip - 1):
        partners.append((here, 2 * lax.rem(chip + step, n_chip) + core))
    partners.append((here, lax.rem(me + n_ac + 2 * core - 1, n_ac)))
    for partner in partners:
        pl.semaphore_signal(barrier, inc=1, device_id=partner, device_id_type=MESH)
    pl.semaphore_wait(barrier, len(partners))

    def block_copies(src, to, slot):
        target = (here, 2 * to + core)
        return (
            pltpu.make_async_remote_copy(
                src_ref=table_ref.at[src], dst_ref=table_ref.at[src],
                send_sem=table_send.at[slot], recv_sem=table_recv.at[src],
                device_id=target, device_id_type=MESH),
            pltpu.make_async_remote_copy(
                src_ref=block_ref.at[src], dst_ref=block_ref.at[src],
                send_sem=block_send.at[slot], recv_sem=block_recv.at[src],
                device_id=target, device_id_type=MESH),
        )

    def row_copies(src, r):
        i, c = peer(r)
        group = here * 2 + core
        target = (i, 2 * chip + c)
        return (
            pltpu.make_async_remote_copy(
                src_ref=tags_ref.at[src, r], dst_ref=got_ref.at[group, src],
                send_sem=tags_send.at[src, r], recv_sem=tags_recv.at[group, src],
                device_id=target, device_id_type=MESH),
            pltpu.make_async_remote_copy(
                src_ref=pack_ref.at[src, r], dst_ref=rows_ref.at[group, src],
                send_sem=rows_send.at[src, r], recv_sem=rows_recv.at[group, src],
                device_id=target, device_id_type=MESH),
        )

    @pl.when(chip > 0)
    def _():
        for item in block_copies(chip, chip - 1, chip):
            item.start()

    @pl.when(chip < n_chip - 1)
    def _():
        for item in block_copies(chip, chip + 1, n_chip):
            item.start()

    width = 128
    above = (lax.broadcasted_iota(jnp.int32, (width, width), 0)
             < lax.broadcasted_iota(jnp.int32, (width, width), 1))
    above = jnp.where(above, 1.0, 0.0).astype(jnp.bfloat16)
    own_group = here * 2 + core
    per = max(1, min(512, plane * capacity) // capacity)

    def select(src):
        r_ids = lax.broadcasted_iota(jnp.int32, (plane, slabs), 0)
        i_ids = here + (r_ids >> 1)
        i_ids = jnp.where(i_ids >= n_les, i_ids - n_les, i_ids)
        ids = i_ids * n_ac + 2 * chip + ((core + r_ids) & 1)
        table = table_ref[src]
        first = ids == table[0:1, :]
        second = ids == table[1:2, :]
        hit = jnp.where(first | second, 1.0, 0.0)
        tag_ref[...] = jnp.where(first, table[2:3, :], jnp.where(second, table[3:4, :], 0))
        offset = jnp.zeros((plane, 1), jnp.float32)
        for k in range(slabs // width):
            part = hit[:, k * width:(k + 1) * width]
            rank = dot(part.astype(jnp.bfloat16), above) + offset
            rank_ref[:, k * width:(k + 1) * width] = jnp.where(
                part > 0.5, rank, -1.0).astype(jnp.int32)
            offset = offset + jnp.sum(part, axis=1, keepdims=True)
        slot = lax.broadcasted_iota(jnp.int32, (capacity, slabs), 0)
        for k in range(plane // per):
            pieces = []
            for q in range(per):
                r = k * per + q
                one = jnp.where(slot == rank_ref[r:r + 1, :], 1.0, 0.0).astype(jnp.bfloat16)
                pieces.append(one)
                tag = tag_ref[r:r + 1, :]
                tag = jnp.concatenate(
                    [(tag >> 5) + 1, tag & 31] + [jnp.zeros_like(tag)] * 6, axis=0)
                found = lax.dot_general(
                    tag.astype(jnp.float32).astype(jnp.bfloat16), one, (((1,), (1,)), ((), ())),
                    preferred_element_type=jnp.float32)
                code = (found[0:1] * 32.0 + found[1:2] - 32.0).astype(jnp.int32)
                code = jnp.broadcast_to(code, (8, capacity))
                if r == 0:
                    got_ref[own_group, src] = code
                else:
                    tags_ref[src, r] = code
            value = dot(jnp.concatenate(pieces, axis=0), block_ref[src]).astype(jnp.bfloat16)
            for q in range(per):
                r = k * per + q
                part = value[q * capacity:(q + 1) * capacity]
                if r == 0:
                    rows_ref[own_group, src] = part
                else:
                    pack_ref[src, r] = part
        for r in range(1, plane):
            for item in row_copies(src, r):
                item.start()

    def source_of(s):
        away = 1 - 2 * lax.rem(s, 2)
        return chip + away * ((s + 1) // 2), chip - away

    def exists(m):
        return jnp.logical_and(m >= 0, m < n_chip)

    def gather(s, carry):
        src, onward = source_of(s)

        @pl.when(exists(src))
        def _():
            @pl.when(s > 0)
            def _():
                for item in block_copies(src, chip, src):
                    item.wait_recv()

                @pl.when(exists(onward))
                def _():
                    for item in block_copies(src, onward, src):
                        item.start()

            select(src)
        return carry

    lax.fori_loop(0, 2 * n_chip - 1, gather, 0)

    def arrived(src, carry):
        for r in range(1, plane):
            i, c = peer(r)
            group = i * 2 + c
            for item in (
                pltpu.make_async_remote_copy(
                    src_ref=tags_ref.at[src, r], dst_ref=got_ref.at[group, src],
                    send_sem=tags_send.at[src, r], recv_sem=tags_recv.at[group, src],
                    device_id=(i, 2 * chip + c), device_id_type=MESH),
                pltpu.make_async_remote_copy(
                    src_ref=pack_ref.at[src, r], dst_ref=rows_ref.at[group, src],
                    send_sem=rows_send.at[src, r], recv_sem=rows_recv.at[group, src],
                    device_id=(i, 2 * chip + c), device_id_type=MESH),
            ):
                item.wait()
        return carry

    lax.fori_loop(0, n_chip, arrived, 0)

    def sent(s, carry):
        src, onward = source_of(s)

        @pl.when(jnp.logical_and(exists(src), exists(onward)))
        def _():
            for item in block_copies(src, onward, src):
                item.wait_send()
        return carry

    lax.fori_loop(1, 2 * n_chip - 1, sent, 0)

    @pl.when(chip > 0)
    def _():
        for item in block_copies(chip, chip - 1, chip):
            item.wait_send()

    @pl.when(chip < n_chip - 1)
    def _():
        for item in block_copies(chip, chip + 1, n_chip):
            item.wait_send()

    for g in range(plane):
        for m in range(n_chip):
            at = (g * n_chip + m) * capacity
            codes_ref[0:1, at:at + capacity] = got_ref[g, m, 0:1, :]
    slots = plane * n_chip * capacity
    chunk = 256

    def combine(k, carry):
        for o in range(NOFF):
            target = lax.broadcasted_iota(jnp.int32, (chunk, slots), 0) + (o * lines + k * chunk)
            one = jnp.where(target == codes_ref[0:1, :], 1.0, 0.0).astype(jnp.bfloat16)
            rows = rows_ref[...].reshape(slots, 3 * coarse)
            got = dot(one, rows).astype(jnp.bfloat16)
            for c in range(3):
                value = dot(got[:, c * coarse:(c + 1) * coarse], weights_ref[o])
                at = (c, pl.ds(k * chunk, chunk))
                if o == 0:
                    source_ref[at] = value
                else:
                    source_ref[at] += value
        return carry

    lax.fori_loop(0, lines // chunk, combine, 0)

    up_line = lines_ref[0, 0]
    down_line = lines_ref[0, 1]
    scale_in = (None, 0.5 * STEP, 0.5 * STEP, STEP)
    scale_out = (STEP / 6.0, STEP / 3.0, STEP / 3.0, STEP / 6.0)
    for f in range(4):
        stage_ref[f, pad:pad + lines, :] = state_ref[f]
    for s in range(4):
        for q, f in enumerate((0, 2)):
            send_ref[s, 0, q:q + 1, :] = stage_ref[f, pl.ds(pad + up_line, 1), :]
            send_ref[s, 1, q:q + 1, :] = stage_ref[f, pl.ds(pad + down_line, 1), :]

        def copy(side, to):
            return pltpu.make_async_remote_copy(
                src_ref=send_ref.at[s, side], dst_ref=ghost_ref.at[s, side],
                send_sem=send_sem.at[s, side], recv_sem=recv_sem.at[s, side],
                device_id={"ac": to}, device_id_type=MESH)

        def dx_of(f):
            dx_ref[f] = dot(stage_ref[f, pad:pad + lines, :].astype(jnp.bfloat16), dmat_ref[...])

        dx_of(0)

        @pl.when(me < n_ac - 1)
        def _():
            copy(0, me + 1).start()

        @pl.when(me > 0)
        def _():
            copy(1, me - 1).start()

        for f in range(1, 4):
            dx_of(f)

        @pl.when(me < n_ac - 1)
        def _():
            copy(0, me + 1).wait_send()
            copy(1, me + 1).wait_recv()

        @pl.when(me > 0)
        def _():
            copy(1, me - 1).wait_send()
            copy(0, me - 1).wait_recv()

        for q, f in enumerate((0, 2)):
            stage_ref[f, pad - 1:pad, :] = ghost_ref[s, 0, q:q + 1, :]
            stage_ref[f, pad + lines:pad + lines + 1, :] = ghost_ref[s, 1, q:q + 1, :]

        def dy(f):
            return (stage_ref[f, pad + 1:pad + 1 + lines, :]
                    - stage_ref[f, pad - 1:pad - 1 + lines, :]) * 0.5

        dy_p = dy(0)
        dy_v = dy(2)

        def finish(f, rate):
            if s == 0:
                total = state_ref[f] + scale_out[s] * rate
            else:
                total = sum_ref[f] + scale_out[s] * rate
            if s == 3:
                out_ref[f] = total
            else:
                sum_ref[f] = total
                stage_ref[f, pad:pad + lines, :] = state_ref[f] + scale_in[s + 1] * rate

        finish(0, -ADVECT * dx_ref[0] - dx_ref[1] - dy_v)
        finish(2, -ADVECT * dx_ref[2] - dy_p - source_ref[1])
        finish(1, -ADVECT * dx_ref[1] - dx_ref[0] - source_ref[0])
        finish(3, -ADVECT * dx_ref[3] - source_ref[2])


def local(velocity, vorticity, cover, target_line, phase, fringe_lines, acoustic):
    n_les = lax.axis_size("les")
    n_ac = lax.axis_size("ac")
    devices = n_les * n_ac
    slabs, coarse = velocity.shape[1:]
    tops = cover.shape[1]
    lines, cells = acoustic.shape[1:]
    capacity = 2 * slabs * tops // devices
    plane, n_chip = 2 * n_les, n_ac // 2
    codes = phase * lines + target_line
    index = jnp.concatenate([cover, codes, cover, codes], axis=1).T
    vmem = pl.BlockSpec(memory_space=pltpu.VMEM)
    dma = pltpu.SemaphoreType.DMA
    return pl.pallas_call(
        functools.partial(step_kernel, capacity),
        out_shape=jax.ShapeDtypeStruct(acoustic.shape, jnp.float32),
        in_specs=[pl.BlockSpec(memory_space=pltpu.SMEM)] + [vmem] * 6,
        out_specs=vmem,
        scratch_shapes=[pltpu.VMEM((3, lines, cells), jnp.float32),
                        pltpu.VMEM((4, lines + 16, cells), jnp.float32),
                        pltpu.VMEM((4, lines, cells), jnp.float32),
                        pltpu.VMEM((4, lines, cells), jnp.float32),
                        pltpu.VMEM((4, 2, 8, cells), jnp.float32),
                        pltpu.VMEM((4, 2, 8, cells), jnp.float32),
                        pltpu.VMEM((n_chip, slabs, 3 * coarse), jnp.bfloat16),
                        pltpu.VMEM((n_chip, 8, slabs), jnp.int32),
                        pltpu.VMEM((n_chip, plane, capacity, 3 * coarse), jnp.bfloat16),
                        pltpu.VMEM((n_chip, plane, 8, capacity), jnp.int32),
                        pltpu.VMEM((plane, n_chip, capacity, 3 * coarse), jnp.bfloat16),
                        pltpu.VMEM((plane, n_chip, 8, capacity), jnp.int32),
                        pltpu.VMEM((8, plane * n_chip * capacity), jnp.int32),
                        pltpu.VMEM((plane, slabs), jnp.int32),
                        pltpu.VMEM((plane, slabs), jnp.int32),
                        dma((4, 2)), dma((4, 2)),
                        dma((n_chip + 1,)), dma((n_chip,)),
                        dma((n_chip + 1,)), dma((n_chip,)),
                        dma((n_chip, plane)), dma((plane, n_chip)),
                        dma((n_chip, plane)), dma((plane, n_chip))],
        compiler_params=pltpu.CompilerParams(
            vmem_limit_bytes=VMEM_LIMIT, collective_id=0, has_side_effects=True),
        name="step",
    )(fringe_lines, velocity, vorticity, index, jnp.asarray(lagrange_table(coarse, cells, NOFF)),
      jnp.asarray(derivative_matrix(cells)), acoustic)


def solution(mesh):
    return jax.shard_map(
        local,
        mesh=mesh,
        in_specs=(
            P(None, ("les", "ac"), None),
            P(None, ("les", "ac"), None),
            P(("les", "ac"), None),
            P(("les", "ac"), None),
            P(("les", "ac"), None),
            P(("les", "ac"), None),
            P(None, ("les", "ac"), None),
        ),
        out_specs=P(None, ("les", "ac"), None),
        check_vma=False,
    )
```

```python
import functools

import jax
import jax.numpy as jnp
import ml_dtypes
import numpy as np
from jax import lax
from jax.experimental import pallas as pl
from jax.experimental.pallas import tpu as pltpu
from jax.sharding import PartitionSpec as P

NOFF = 4
ADVECT = 0.5
STEP = 0.4
MESH = pl.DeviceIdType.MESH
VMEM_LIMIT = 60 * 1024 * 1024


def lagrange_table(coarse, fine, phases):
    fine_ids = np.arange(fine)
    phase_ids = np.arange(phases)
    numerator = phases * fine_ids[None, :] + phase_ids[:, None]
    first_tap = np.clip(numerator // (2 * phases) - 1, 0, coarse - 4)
    where_x = numerator / (2.0 * phases)
    lagrange = np.zeros((phases, coarse, fine))
    for tap in range(4):
        weight = np.ones_like(where_x)
        for other in range(4):
            if other != tap:
                weight = weight * (where_x - (first_tap + other)) / float(tap - other)
        hit = np.arange(coarse)[None, :, None] == (first_tap + tap)[:, None, :]
        lagrange = lagrange + np.where(hit, weight[:, None, :], 0.0)
    return lagrange.astype(np.float32).astype(ml_dtypes.bfloat16)


def derivative_matrix(cells):
    ids = np.arange(cells)
    distance = ids[:, None] - ids[None, :]
    rhs = np.where(distance == -1, 0.75, np.where(distance == 1, -0.75, 0.0))
    lhs = np.where(distance == 0, 1.0, np.where(np.abs(distance) == 1, 0.25, 0.0))
    return np.linalg.solve(lhs, rhs).T.astype(np.float32).astype(ml_dtypes.bfloat16)


def dot(a, b):
    return jnp.dot(a, b, preferred_element_type=jnp.float32)


def step_kernel(capacity, lines_ref, vel_ref, vort_ref, index_ref, weights_ref, dmat_ref, state_ref,
                out_ref, source_ref, stage_ref, dx_ref, sum_ref, send_ref, ghost_ref,
                block_ref, table_ref, pack_ref, tags_ref, rows_ref, got_ref, codes_ref, acc_ref,
                rank_ref, tag_ref, send_sem, recv_sem,
                block_send, block_recv, table_send, table_recv,
                rows_send, rows_recv, tags_send, tags_recv):
    n_les = lax.axis_size("les")
    n_ac = lax.axis_size("ac")
    n_chip = n_ac // 2
    here = lax.axis_index("les")
    me = lax.axis_index("ac")
    chip = me // 2
    core = lax.rem(me, 2)
    lines = state_ref.shape[1]
    cells = state_ref.shape[2]
    slabs = vel_ref.shape[1]
    coarse = weights_ref.shape[1]
    plane = 2 * n_les
    pad = 8
    ghost_ref[...] = jnp.zeros_like(ghost_ref)
    send_ref[...] = jnp.zeros_like(send_ref)
    vel = [vel_ref[c].astype(jnp.float32) for c in range(3)]
    vor = [vort_ref[c].astype(jnp.float32) for c in range(3)]
    for c in range(3):
        a, b = (c + 1) % 3, (c + 2) % 3
        block_ref[chip, :, c * coarse:(c + 1) * coarse] = (
            vor[a] * vel[b] - vor[b] * vel[a]).astype(jnp.bfloat16)
    table_ref[chip] = index_ref[...]

    def peer(r):
        return lax.rem(here + r // 2, n_les), lax.rem(core + r % 2, 2)

    barrier = pltpu.get_barrier_semaphore()
    partners = []
    for r in range(1, plane):
        i, c = peer(r)
        partners.append((i, 2 * chip + c))
    for step in (1, n_chip - 1):
        partners.append((here, 2 * lax.rem(chip + step, n_chip) + core))
    partners.append((here, lax.rem(me + n_ac + 2 * core - 1, n_ac)))
    for partner in partners:
        pl.semaphore_signal(barrier, inc=1, device_id=partner, device_id_type=MESH)
    pl.semaphore_wait(barrier, len(partners))

    def block_copies(src, to, slot):
        target = (here, 2 * to + core)
        return (
            pltpu.make_async_remote_copy(
                src_ref=table_ref.at[src], dst_ref=table_ref.at[src],
                send_sem=table_send.at[slot], recv_sem=table_recv.at[src],
                device_id=target, device_id_type=MESH),
            pltpu.make_async_remote_copy(
                src_ref=block_ref.at[src], dst_ref=block_ref.at[src],
                send_sem=block_send.at[slot], recv_sem=block_recv.at[src],
                device_id=target, device_id_type=MESH),
        )

    def row_copies(src, r):
        i, c = peer(r)
        group = here * 2 + core
        target = (i, 2 * chip + c)
        return (
            pltpu.make_async_remote_copy(
                src_ref=tags_ref.at[src, r], dst_ref=got_ref.at[src, group],
                send_sem=tags_send.at[src, r], recv_sem=tags_recv.at[group, src],
                device_id=target, device_id_type=MESH),
            pltpu.make_async_remote_copy(
                src_ref=pack_ref.at[src, r], dst_ref=rows_ref.at[src, group],
                send_sem=rows_send.at[src, r], recv_sem=rows_recv.at[group, src],
                device_id=target, device_id_type=MESH),
        )

    @pl.when(chip > 0)
    def _():
        for item in block_copies(chip, chip - 1, chip):
            item.start()

    @pl.when(chip < n_chip - 1)
    def _():
        for item in block_copies(chip, chip + 1, n_chip):
            item.start()

    width = 128
    above = (lax.broadcasted_iota(jnp.int32, (width, width), 0)
             < lax.broadcasted_iota(jnp.int32, (width, width), 1))
    above = jnp.where(above, 1.0, 0.0).astype(jnp.bfloat16)
    own_group = here * 2 + core
    per = max(1, min(512, plane * capacity) // capacity)

    def select(src):
        r_ids = lax.broadcasted_iota(jnp.int32, (plane, slabs), 0)
        i_ids = here + (r_ids >> 1)
        i_ids = jnp.where(i_ids >= n_les, i_ids - n_les, i_ids)
        ids = i_ids * n_ac + 2 * chip + ((core + r_ids) & 1)
        table = table_ref[src]
        first = ids == table[0:1, :]
        second = ids == table[1:2, :]
        hit = jnp.where(first | second, 1.0, 0.0)
        tag_ref[...] = jnp.where(first, table[2:3, :], jnp.where(second, table[3:4, :], 0))
        offset = jnp.zeros((plane, 1), jnp.float32)
        for k in range(slabs // width):
            part = hit[:, k * width:(k + 1) * width]
            rank = dot(part.astype(jnp.bfloat16), above) + offset
            rank_ref[:, k * width:(k + 1) * width] = jnp.where(
                part > 0.5, rank, -1.0).astype(jnp.int32)
            offset = offset + jnp.sum(part, axis=1, keepdims=True)
        slot = lax.broadcasted_iota(jnp.int32, (capacity, slabs), 0)
        for k in range(plane // per):
            pieces = []
            for q in range(per):
                r = k * per + q
                one = jnp.where(slot == rank_ref[r:r + 1, :], 1.0, 0.0).astype(jnp.bfloat16)
                pieces.append(one)
                tag = tag_ref[r:r + 1, :]
                tag = jnp.concatenate(
                    [(tag >> 5) + 1, tag & 31] + [jnp.zeros_like(tag)] * 6, axis=0)
                found = lax.dot_general(
                    tag.astype(jnp.float32).astype(jnp.bfloat16), one, (((1,), (1,)), ((), ())),
                    preferred_element_type=jnp.float32)
                code = (found[0:1] * 32.0 + found[1:2] - 32.0).astype(jnp.int32)
                code = jnp.broadcast_to(code, (8, capacity))
                if r == 0:
                    got_ref[src, own_group] = code
                else:
                    tags_ref[src, r] = code
            value = dot(jnp.concatenate(pieces, axis=0), block_ref[src]).astype(jnp.bfloat16)
            for q in range(per):
                r = k * per + q
                part = value[q * capacity:(q + 1) * capacity]
                if r == 0:
                    rows_ref[src, own_group] = part
                else:
                    pack_ref[src, r] = part
        for r in range(1, plane):
            for item in row_copies(src, r):
                item.start()

    def source_of(s):
        away = 1 - 2 * lax.rem(s, 2)
        return chip + away * ((s + 1) // 2), chip - away

    def exists(m):
        return jnp.logical_and(m >= 0, m < n_chip)

    chunk = 256
    lag = 2
    acc_ref[...] = jnp.zeros_like(acc_ref)

    def arrived(src):
        for r in range(1, plane):
            i, c = peer(r)
            group = i * 2 + c
            for item in (
                pltpu.make_async_remote_copy(
                    src_ref=tags_ref.at[src, r], dst_ref=got_ref.at[src, group],
                    send_sem=tags_send.at[src, r], recv_sem=tags_recv.at[group, src],
                    device_id=(i, 2 * chip + c), device_id_type=MESH),
                pltpu.make_async_remote_copy(
                    src_ref=pack_ref.at[src, r], dst_ref=rows_ref.at[src, group],
                    send_sem=rows_send.at[src, r], recv_sem=rows_recv.at[group, src],
                    device_id=(i, 2 * chip + c), device_id_type=MESH),
            ):
                item.wait()
        for g in range(plane):
            codes_ref[0:1, g * capacity:(g + 1) * capacity] = got_ref[src, g, 0:1, :]
        slots = plane * capacity

        def add(k, carry):
            at = pl.ds(k * chunk, chunk)
            target = lax.broadcasted_iota(jnp.int32, (chunk, slots), 0) + k * chunk
            one = jnp.where(target == codes_ref[0:1, :], 1.0, 0.0).astype(jnp.bfloat16)
            acc_ref[at, :] += dot(one, rows_ref[src].reshape(slots, 3 * coarse))
            return carry

        lax.fori_loop(0, NOFF * lines // chunk, add, 0)

    def gather(s, carry):
        src, onward = source_of(s)

        @pl.when(jnp.logical_and(exists(src), s < 2 * n_chip - 1))
        def _():
            @pl.when(s > 0)
            def _():
                for item in block_copies(src, chip, src):
                    item.wait_recv()

                @pl.when(exists(onward))
                def _():
                    for item in block_copies(src, onward, src):
                        item.start()

            select(src)

        before, _ = source_of(jnp.maximum(s - lag, 0))

        @pl.when(jnp.logical_and(s >= lag, exists(before)))
        def _():
            arrived(before)
        return carry

    lax.fori_loop(0, 2 * n_chip - 1 + lag, gather, 0)

    def sent(s, carry):
        src, onward = source_of(s)

        @pl.when(jnp.logical_and(exists(src), exists(onward)))
        def _():
            for item in block_copies(src, onward, src):
                item.wait_send()
        return carry

    lax.fori_loop(1, 2 * n_chip - 1, sent, 0)

    @pl.when(chip > 0)
    def _():
        for item in block_copies(chip, chip - 1, chip):
            item.wait_send()

    @pl.when(chip < n_chip - 1)
    def _():
        for item in block_copies(chip, chip + 1, n_chip):
            item.wait_send()

    def combine(k, carry):
        for o in range(NOFF):
            got = acc_ref[pl.ds(o * lines + k * chunk, chunk), :].astype(jnp.bfloat16)
            for c in range(3):
                value = dot(got[:, c * coarse:(c + 1) * coarse], weights_ref[o])
                at = (c, pl.ds(k * chunk, chunk))
                if o == 0:
                    source_ref[at] = value
                else:
                    source_ref[at] += value
        return carry

    lax.fori_loop(0, lines // chunk, combine, 0)

    up_line = lines_ref[0, 0]
    down_line = lines_ref[0, 1]
    scale_in = (None, 0.5 * STEP, 0.5 * STEP, STEP)
    scale_out = (STEP / 6.0, STEP / 3.0, STEP / 3.0, STEP / 6.0)
    for f in range(4):
        stage_ref[f, pad:pad + lines, :] = state_ref[f]
    for s in range(4):
        for q, f in enumerate((0, 2)):
            send_ref[s, 0, q:q + 1, :] = stage_ref[f, pl.ds(pad + up_line, 1), :]
            send_ref[s, 1, q:q + 1, :] = stage_ref[f, pl.ds(pad + down_line, 1), :]

        def copy(side, to):
            return pltpu.make_async_remote_copy(
                src_ref=send_ref.at[s, side], dst_ref=ghost_ref.at[s, side],
                send_sem=send_sem.at[s, side], recv_sem=recv_sem.at[s, side],
                device_id={"ac": to}, device_id_type=MESH)

        def dx_of(f):
            dx_ref[f] = dot(stage_ref[f, pad:pad + lines, :].astype(jnp.bfloat16), dmat_ref[...])

        dx_of(0)

        @pl.when(me < n_ac - 1)
        def _():
            copy(0, me + 1).start()

        @pl.when(me > 0)
        def _():
            copy(1, me - 1).start()

        for f in range(1, 4):
            dx_of(f)

        @pl.when(me < n_ac - 1)
        def _():
            copy(0, me + 1).wait_send()
            copy(1, me + 1).wait_recv()

        @pl.when(me > 0)
        def _():
            copy(1, me - 1).wait_send()
            copy(0, me - 1).wait_recv()

        for q, f in enumerate((0, 2)):
            stage_ref[f, pad - 1:pad, :] = ghost_ref[s, 0, q:q + 1, :]
            stage_ref[f, pad + lines:pad + lines + 1, :] = ghost_ref[s, 1, q:q + 1, :]

        def dy(f):
            return (stage_ref[f, pad + 1:pad + 1 + lines, :]
                    - stage_ref[f, pad - 1:pad - 1 + lines, :]) * 0.5

        dy_p = dy(0)
        dy_v = dy(2)

        def finish(f, rate):
            if s == 0:
                total = state_ref[f] + scale_out[s] * rate
            else:
                total = sum_ref[f] + scale_out[s] * rate
            if s == 3:
                out_ref[f] = total
            else:
                sum_ref[f] = total
                stage_ref[f, pad:pad + lines, :] = state_ref[f] + scale_in[s + 1] * rate

        finish(0, -ADVECT * dx_ref[0] - dx_ref[1] - dy_v)
        finish(2, -ADVECT * dx_ref[2] - dy_p - source_ref[1])
        finish(1, -ADVECT * dx_ref[1] - dx_ref[0] - source_ref[0])
        finish(3, -ADVECT * dx_ref[3] - source_ref[2])


def local(velocity, vorticity, cover, target_line, phase, fringe_lines, acoustic):
    n_les = lax.axis_size("les")
    n_ac = lax.axis_size("ac")
    devices = n_les * n_ac
    slabs, coarse = velocity.shape[1:]
    tops = cover.shape[1]
    lines, cells = acoustic.shape[1:]
    capacity = 2 * slabs * tops // devices
    plane, n_chip = 2 * n_les, n_ac // 2
    codes = phase * lines + target_line
    index = jnp.concatenate([cover, codes, cover, codes], axis=1).T
    vmem = pl.BlockSpec(memory_space=pltpu.VMEM)
    dma = pltpu.SemaphoreType.DMA
    return pl.pallas_call(
        functools.partial(step_kernel, capacity),
        out_shape=jax.ShapeDtypeStruct(acoustic.shape, jnp.float32),
        in_specs=[pl.BlockSpec(memory_space=pltpu.SMEM)] + [vmem] * 6,
        out_specs=vmem,
        scratch_shapes=[pltpu.VMEM((3, lines, cells), jnp.float32),
                        pltpu.VMEM((4, lines + 16, cells), jnp.float32),
                        pltpu.VMEM((4, lines, cells), jnp.float32),
                        pltpu.VMEM((4, lines, cells), jnp.float32),
                        pltpu.VMEM((4, 2, 8, cells), jnp.float32),
                        pltpu.VMEM((4, 2, 8, cells), jnp.float32),
                        pltpu.VMEM((n_chip, slabs, 3 * coarse), jnp.bfloat16),
                        pltpu.VMEM((n_chip, 8, slabs), jnp.int32),
                        pltpu.VMEM((n_chip, plane, capacity, 3 * coarse), jnp.bfloat16),
                        pltpu.VMEM((n_chip, plane, 8, capacity), jnp.int32),
                        pltpu.VMEM((n_chip, plane, capacity, 3 * coarse), jnp.bfloat16),
                        pltpu.VMEM((n_chip, plane, 8, capacity), jnp.int32),
                        pltpu.VMEM((8, plane * capacity), jnp.int32),
                        pltpu.VMEM((NOFF * lines, 3 * coarse), jnp.float32),
                        pltpu.VMEM((plane, slabs), jnp.int32),
                        pltpu.VMEM((plane, slabs), jnp.int32),
                        dma((4, 2)), dma((4, 2)),
                        dma((n_chip + 1,)), dma((n_chip,)),
                        dma((n_chip + 1,)), dma((n_chip,)),
                        dma((n_chip, plane)), dma((plane, n_chip)),
                        dma((n_chip, plane)), dma((plane, n_chip))],
        compiler_params=pltpu.CompilerParams(
            vmem_limit_bytes=VMEM_LIMIT, collective_id=0, has_side_effects=True),
        name="step",
    )(fringe_lines, velocity, vorticity, index, jnp.asarray(lagrange_table(coarse, cells, NOFF)),
      jnp.asarray(derivative_matrix(cells)), acoustic)


def solution(mesh):
    return jax.shard_map(
        local,
        mesh=mesh,
        in_specs=(
            P(None, ("les", "ac"), None),
            P(None, ("les", "ac"), None),
            P(("les", "ac"), None),
            P(("les", "ac"), None),
            P(("les", "ac"), None),
            P(("les", "ac"), None),
            P(None, ("les", "ac"), None),
        ),
        out_specs=P(None, ("les", "ac"), None),
        check_vma=False,
    )
```
